32 devices in a mesh: dp: 2 (over x), blk: 4 (over z), ulysses: 4 (over y, core).
Axes of the slice: x: 2, y: 2, z: 4, core: 2. Of those that a mesh axis runs over, the one named last changes fastest.
Arguments:
- inputs: bfloat16 [2, 2, 1024, 2048], P(None, 'dp', ('blk', 'ulysses')), may hold values from -6 to 6
- gain_attn: float32 [2048], replicated, may hold values from 0.5 to 1.5
- w_qkv: bfloat16 [2048, 6144], P(('dp', 'blk', 'ulysses')), may hold values from -0.1875 to 0.1875
- w_out: bfloat16 [2048, 2048], P(('dp', 'blk', 'ulysses')), may hold values from -0.5 to 0.5
- gain_mlp: float32 [2048], replicated, may hold values from 0.5 to 1.5
- w_up: bfloat16 [2048, 8192], P(('dp', 'blk', 'ulysses')), may hold values from -0.125 to 0.125
- w_down: bfloat16 [8192, 2048], P(('dp', 'blk', 'ulysses')), may hold values from -0.0625 to 0.0625
- doc_lengths: int32 [2, 2, 8], P(None, 'dp'), may hold values from 1 to 512, 1024 in all within a row
- cotangent: bfloat16 [2, 2, 1024, 2048], P(None, 'dp', ('blk', 'ulysses')), may hold values from -6 to 6
Outputs:
- output: bfloat16 [2, 2, 1024, 2048], P(None, 'dp', ('blk', 'ulysses'))
- input_grad: float32 [2, 2, 1024, 2048], P(None, 'dp', ('blk', 'ulysses'))
- grad_gain_attn: float32 [2048], P(('dp', 'blk', 'ulysses'))
- grad_w_qkv: float32 [2048, 6144], P(('dp', 'blk', 'ulysses'))
- grad_w_out: float32 [2048, 2048], P(('dp', 'blk', 'ulysses'))
- grad_gain_mlp: float32 [2048], P(('dp', 'blk', 'ulysses'))
- grad_w_up: float32 [2048, 8192], P(('dp', 'blk', 'ulysses'))
- grad_w_down: float32 [8192, 2048], P(('dp', 'blk', 'ulysses'))
The draws below stay inside these ranges and needn't reach their ends.
Inputs may be any that keep to these rules, and one draw needn't show every extreme that they name: `doc_lengths`: each stream's 8 lengths sum to 1024, and its longest document has 512 positions.
All inputs are finite; a program needn't handle non-finite values.
Results may differ from the reference program's by a relative error of at most 0.015.
Values may be sent and summed in bfloat16 or wider, within the bound.
No kernel may reach another device: no remote copies, remote signals or barrier semaphores. Data moves between devices by JAX's collectives and lax.ppermute only.
A program may use at most 704 MiB of HBM per device.

```python
import math
import jax
import jax.numpy as jnp
import numpy as np
from jax import lax

D = 2048
HEADS = 16
HEAD_DIM = 128
FF = 8192
MB = 2
NDOC = 8
SEQ = 1024
N_DP = 2


def block_scale(stream_key, dims, split, least, largest):
    level, own = 1.0, jax.random.fold_in(stream_key, 6)
    for axis_at, shards_of in split:
        heights = jnp.exp(jax.random.uniform(jax.random.fold_in(own, axis_at), (shards_of,), jnp.float32, least / len(split), largest / len(split)))
        level = level * jnp.repeat(heights, dims[axis_at] // shards_of).reshape([-1 if axis == axis_at else 1 for axis in range(len(dims))])
    return level


def length_profile(number_of, total, reach, skew):
    weights = [(1 << 20) // math.isqrt(standing ** skew) + 1 for standing in range(2, number_of + 1)]
    surplus, counts = total - reach - (number_of - 1), [1] * (number_of - 1)
    while surplus > 0:
        candidates = [i for i in range(number_of - 1) if counts[i] < reach]
        mass, left = sum([weights[i] for i in candidates]), surplus
        for i in candidates:
            addition = min(reach - counts[i], max(1, left * weights[i] // mass), surplus)
            counts[i] = counts[i] + addition
            surplus = surplus - addition
    return np.array([reach] + counts)


def uneven_parts(own_key, amount, total, limit, lean):
    if amount == 2:
        one = jax.random.randint(own_key, (), max(1, total - limit), min(limit, total - 1) + 1)
        return jnp.stack([one, total - one])
    sizes = jnp.asarray(length_profile(amount, total, limit, lean), jnp.int32)
    twos = (amount - 1) // 2
    giver, sink = sizes[1:1 + 2 * twos:2], sizes[2:2 + 2 * twos:2]
    slack = jnp.minimum(giver - 1, limit - sink)
    moved = jax.random.randint(jax.random.fold_in(own_key, 1), (twos,), 0, 1 << 20) % (slack + 1)
    sizes = sizes.at[1:1 + 2 * twos:2].set(giver - moved).at[2:2 + 2 * twos:2].set(sink + moved)
    return sizes[jax.random.permutation(jax.random.fold_in(own_key, 2), amount)]


def centred(own_key, extent, scale, most, split=(), kind=jnp.bfloat16):
    level = block_scale(own_key, extent, split, -0.22, 0.18) if split else 1.0
    values = jax.random.normal(own_key, extent, jnp.float32) * scale * level
    return jnp.minimum(jnp.maximum(values, -most), most).astype(kind)


def setup_inputs(seed: int = 0) -> dict:
    key_of = jax.random.split(jax.random.key(seed), 10)
    return {
        "inputs": centred(key_of[0], (MB, N_DP, SEQ, D), 1.0, 6.0, ((1, 2), (2, 16))),
        "gain_attn": jnp.clip(1.0 + 0.1 * jax.random.normal(key_of[1], (D,), jnp.float32), 0.5, 1.5),
        "w_qkv": centred(key_of[2], (D, 3 * D), (D // 2) ** -0.5, 0.1875, ((0, 32),)),
        "w_out": centred(key_of[3], (D, D), (D // 16) ** -0.5, 0.5, ((0, 32),)),
        "gain_mlp": jnp.clip(1.0 + 0.1 * jax.random.normal(key_of[4], (D,), jnp.float32), 0.5, 1.5),
        "w_up": centred(key_of[5], (D, FF), D ** -0.5, 0.125, ((0, 32),)),
        "w_down": centred(key_of[6], (FF, D), FF ** -0.5, 0.0625, ((0, 32),)),
        "doc_lengths": jax.vmap(lambda own: uneven_parts(own, NDOC, SEQ, SEQ // 2, 2))(jax.random.split(key_of[7], MB * N_DP)).reshape((MB, N_DP, NDOC)).astype(jnp.int32),
        "cotangent": centred(key_of[8], (MB, N_DP, SEQ, D), 1.0, 6.0, ((1, 2), (2, 16))),
    }


@jax.custom_vjp
def low(v):
    return lax.optimization_barrier(v.astype(jnp.bfloat16)).astype(jnp.float32)

@jax.custom_vjp
def low_back(v):
    return v

def low_keep(v):
    return (low(v), None)

def low_pass(kept, grad):
    return (grad,)

def back_keep(v):
    return (v, None)

def back_low(kept, grad):
    return (low(grad),)
low.defvjp(low_keep, low_pass)
low_back.defvjp(back_keep, back_low)
highest = lax.Precision.HIGHEST
epsilon = 1e-05

def normalize(field, gain_vector):
    centered = field - lax.optimization_barrier(jnp.mean(field, axis=-1, keepdims=True))
    variance = lax.optimization_barrier(jnp.mean(centered * centered, axis=-1, keepdims=True))
    return centered * lax.rsqrt(variance + epsilon) * gain_vector

def document_ids(lengths):
    starts = jnp.cumsum(lengths) - lengths
    positions = jnp.arange(SEQ, dtype=jnp.int32)
    return lax.optimization_barrier(jnp.sum((positions[:, None] >= starts[None, 1:]).astype(jnp.int32), axis=1))

def layer(stream_in, gain_attn, w_qkv, w_out, gain_mlp, w_up, w_down, allowed):
    normed_one = low(normalize(stream_in, gain_attn))
    projected = low(low_back(jnp.dot(normed_one, w_qkv, precision=highest)))
    split_heads = projected.reshape(SEQ, 3, HEADS, HEAD_DIM).transpose(1, 2, 0, 3)
    score_scale = HEAD_DIM ** (-0.5)

    def one_head(operands):
        queries, key_rows, value_rows = operands
        scores = low_back(score_scale * jnp.dot(queries, key_rows.T, precision=highest))
        scores = jnp.where(allowed, scores, -1e+30)
        probabilities = jax.nn.softmax(scores, axis=-1)
        return jnp.dot(low(probabilities), value_rows, precision=highest)
    attended = lax.map(jax.checkpoint(one_head), (split_heads[0], split_heads[1], split_heads[2]))
    attended = low(low_back(attended.transpose(1, 0, 2).reshape(SEQ, D)))
    middle = stream_in + low_back(jnp.dot(attended, w_out, precision=highest))
    normed_two = low(normalize(middle, gain_mlp))
    up_proj = low_back(jnp.dot(normed_two, w_up, precision=highest))
    activated = low(jax.nn.gelu(up_proj, approximate=True))
    return middle + low_back(jnp.dot(activated, w_down, precision=highest))

def reference(inputs, gain_attn, w_qkv, w_out, gain_mlp, w_up, w_down, doc_lengths, cotangent):
    params = (gain_attn.astype(jnp.float32), w_qkv.astype(jnp.float32), w_out.astype(jnp.float32), gain_mlp.astype(jnp.float32), w_up.astype(jnp.float32), w_down.astype(jnp.float32))
    streams = inputs.astype(jnp.float32).reshape(MB * N_DP, SEQ, D)
    cotangents = cotangent.astype(jnp.float32).reshape(MB * N_DP, SEQ, D)
    lengths_all = doc_lengths.reshape(MB * N_DP, NDOC)
    positions = jnp.arange(SEQ, dtype=jnp.int32)

    def one_stream(totals, operands):
        stream_in, stream_cot, lengths = operands
        doc_ids = document_ids(lengths)
        allowed = (doc_ids[:, None] == doc_ids[None, :]) & (positions[None, :] <= positions[:, None])

        def forward(field, gain_one, weight_qkv, weight_out, gain_two, weight_up, weight_down):
            return layer(field, gain_one, weight_qkv, weight_out, gain_two, weight_up, weight_down, allowed)
        result, backward = jax.vjp(forward, stream_in, params[0], params[1], params[2], params[3], params[4], params[5])
        grads = backward(stream_cot)
        totals = tuple((total_now + grad_now for total_now, grad_now in zip(totals, grads[1:])))
        return (totals, (result.astype(jnp.bfloat16), grads[0]))
    zeros_start = tuple((jnp.zeros(weight_now.shape, jnp.float32) for weight_now in params))
    sums, (results, input_grads) = lax.scan(one_stream, zeros_start, (streams, cotangents, lengths_all))
    return (results.reshape(MB, N_DP, SEQ, D), input_grads.reshape(MB, N_DP, SEQ, D), sums[0], sums[1], sums[2], sums[3], sums[4], sums[5])
```

```python
import math

import jax
import jax.numpy as jnp
from jax import lax
from jax.sharding import Mesh
from jax.sharding import PartitionSpec as P

HEADS = 16
HEAD_DIM = 128
epsilon = 1e-05
bf16 = jnp.bfloat16
f32 = jnp.float32

J = ("zb", "u")
G = ("dp", "rep", "mb")
ALL = ("dp", "rep", "zb", "mb", "u")


def normalize(field):
    centered = field - jnp.mean(field, axis=-1, keepdims=True)
    inv_std = lax.rsqrt(jnp.mean(centered * centered, axis=-1, keepdims=True) + epsilon)
    return centered * inv_std, inv_std


def norm_back(grad_out, normed, inv_std, gain_vector):
    scaled = grad_out * gain_vector
    mean_one = jnp.mean(scaled, axis=-1, keepdims=True)
    mean_two = jnp.mean(scaled * normed, axis=-1, keepdims=True)
    return inv_std * (scaled - mean_one - normed * mean_two)


def document_ids(lengths, positions):
    starts = jnp.cumsum(lengths) - lengths
    return jnp.sum((positions[:, None] >= starts[None, 1:]).astype(jnp.int32), axis=1)


def times(left, right):
    return jnp.dot(left, right, preferred_element_type=f32)


def times_transposed(left, right):
    return lax.dot_general(left, right, (((1,), (1,)), ((), ())), preferred_element_type=f32)


def rows_product(left, right):
    return lax.dot_general(left, right, (((0,), (0,)), ((), ())), preferred_element_type=f32)


def gather(field, axes):
    return lax.all_gather(field, axes, axis=0, tiled=True)


def scatter(field, axes):
    return lax.psum_scatter(field, axes, scatter_dimension=0, tiled=True)


def exchange(field, axes, split, concat):
    return lax.all_to_all(field, axes, split, concat, tiled=True)


def on_device(inputs, gain_attn, w_qkv, w_out, gain_mlp, w_up, w_down, doc_lengths, cotangent):
    size = {name: lax.axis_size(name) for name in ALL}
    n_dr = size["dp"] * size["rep"]
    n_zb, n_mb, n_u = size["zb"], size["mb"], size["u"]
    n_g = n_dr * n_mb
    n_j = n_zb * n_u
    rows = w_qkv.shape[0]
    width = w_qkv.shape[0] * n_g * n_j
    hidden = w_up.shape[1]
    rows_down = w_down.shape[0]
    heads_here = HEADS // n_j
    cols = heads_here * HEAD_DIM
    piece = inputs.shape[2]
    tokens = n_mb * piece
    group = n_j * tokens

    qkv_cols = exchange(w_qkv.reshape(rows, 3, n_j, cols), J, 2, 0).reshape(n_j * rows, 3 * cols)
    up_send = w_up.reshape(rows, n_dr, n_zb, n_mb, n_u, rows_down).transpose(2, 4, 0, 1, 3, 5)
    up_cols = exchange(up_send.reshape(n_j * rows, n_g * rows_down), J, 0, 0)

    def natural_rows(field):
        lead = field.reshape(n_dr, n_mb, n_zb, n_u * rows, field.shape[1])
        return lead.transpose(0, 2, 1, 3, 4).reshape(width, field.shape[1])

    def owner_rows(field):
        lead = field.reshape(n_dr, n_zb, n_mb, n_u * rows, field.shape[1])
        return lead.transpose(0, 2, 1, 3, 4).reshape(width, field.shape[1])

    qkv_here = natural_rows(gather(qkv_cols, G))
    out_all = gather(w_out, ALL)
    up_here = natural_rows(gather(up_cols, G))
    down_here = gather(w_down, G)

    stream_in = exchange(inputs[:, 0], "mb", 0, 0).reshape(tokens, width).astype(f32)
    grad_down = exchange(cotangent[:, 0], "mb", 0, 0).reshape(tokens, width)
    cot_all = gather(grad_down, J)
    lengths = lax.dynamic_index_in_dim(doc_lengths[:, 0], lax.axis_index("mb"), 0, keepdims=False)

    normed_first, inv_first = normalize(stream_in)
    normed_one = gather((normed_first * gain_attn).astype(bf16), J)
    qkv = times(normed_one, qkv_here).astype(bf16)

    place = lax.broadcasted_iota(jnp.int32, (n_zb, n_mb, n_u, piece), 0) * (n_mb * n_u * piece)
    place = place + lax.broadcasted_iota(jnp.int32, place.shape, 1) * (n_u * piece)
    place = place + lax.broadcasted_iota(jnp.int32, place.shape, 2) * piece
    place = place + lax.broadcasted_iota(jnp.int32, place.shape, 3)
    place = place.transpose(0, 2, 1, 3).reshape(group)
    query_pos = place + lax.axis_index("rep") * group
    key_pos = jnp.concatenate([place + turn * group for turn in range(size["rep"])])
    query_doc = document_ids(lengths, query_pos)
    key_doc = document_ids(lengths, key_pos)
    allowed = (query_doc[:, None] == key_doc[None, :]) & (key_pos[None, :] <= query_pos[:, None])

    heads = qkv.reshape(group, 3, heads_here, HEAD_DIM)
    queries = heads[:, 0]
    keys = heads[:, 1]
    values = heads[:, 2]
    if size["rep"] > 1:
        keys = gather(keys, "rep")
        values = gather(values, "rep")
    score_scale = HEAD_DIM ** (-0.5)
    scores = jnp.einsum("qhd,khd->hqk", queries, keys, preferred_element_type=f32) * score_scale
    scores = jnp.where(allowed[None], scores, -1e30)
    row_max = jnp.max(scores, axis=-1, keepdims=True)
    weights = jnp.exp(scores - row_max)
    probs = weights / jnp.sum(weights, axis=-1, keepdims=True)
    probs_low = probs.astype(bf16)
    attended_full = jnp.einsum("hqk,khd->qhd", probs_low, values, preferred_element_type=f32)
    attended_here = attended_full.reshape(group, cols).astype(bf16)
    attended = exchange(attended_here, J, 0, 1)
    middle = stream_in + times(attended, out_all)

    normed_second, inv_second = normalize(middle)
    normed_two = gather((normed_second * gain_mlp).astype(bf16), J)
    up_proj = times(normed_two, up_here)
    activated_full, gelu_back = jax.vjp(lambda field: jax.nn.gelu(field, approximate=True), up_proj)
    activated = activated_full.astype(bf16)
    grad_up = gelu_back(times_transposed(cot_all, down_here))[0].astype(bf16)
    grad_two = scatter(times_transposed(grad_up, up_here).astype(bf16), J).astype(f32)
    result = middle + scatter(times(activated, down_here).astype(bf16), J).astype(f32)
    output = exchange(result.astype(bf16).reshape(n_mb, piece, width), "mb", 0, 0)

    grad_middle = grad_down.astype(f32) + norm_back(grad_two, normed_second, inv_second, gain_mlp)
    grad_branch = grad_middle.astype(bf16)
    grad_attended = times_transposed(grad_branch, out_all).astype(bf16)
    grad_out = exchange(grad_attended, J, 1, 0).reshape(group, heads_here, HEAD_DIM)
    row_dots = jnp.sum(grad_out.astype(f32) * attended_full, axis=-1).T
    grad_values = jnp.einsum("hqk,qhd->khd", probs_low, grad_out, preferred_element_type=f32)
    grad_probs = jnp.einsum("qhd,khd->hqk", grad_out, values, preferred_element_type=f32)
    grad_scores = (probs * (grad_probs - row_dots[:, :, None])).astype(bf16)
    grad_queries = jnp.einsum("hqk,khd->qhd", grad_scores, keys, preferred_element_type=f32)
    grad_keys = jnp.einsum("hqk,qhd->khd", grad_scores, queries, preferred_element_type=f32)
    grad_queries = (grad_queries * score_scale).astype(bf16)
    grad_keys = (grad_keys * score_scale).astype(bf16)
    grad_values = grad_values.astype(bf16)
    if size["rep"] > 1:
        grad_keys = scatter(grad_keys, "rep")
        grad_values = scatter(grad_values, "rep")
    grad_qkv = jnp.stack([grad_queries, grad_keys, grad_values], axis=1).reshape(group, 3 * cols)
    grad_one = scatter(times_transposed(grad_qkv, qkv_here).astype(bf16), J).astype(f32)
    input_grad = grad_middle + norm_back(grad_one, normed_first, inv_first, gain_attn)
    input_grad = exchange(input_grad.astype(bf16).reshape(n_mb, piece, width), "mb", 0, 0)

    part_up = owner_rows(rows_product(normed_two, grad_up).astype(bf16))
    own_up = exchange(scatter(part_up, G), J, 0, 0)
    own_up = own_up.reshape(n_zb, n_u, rows, n_dr, n_mb, rows_down).transpose(2, 3, 0, 4, 1, 5)
    grad_w_up = own_up.reshape(rows, hidden).astype(f32)
    grad_w_down = scatter(rows_product(activated, cot_all).astype(bf16), G).astype(f32)
    branch_all = gather(grad_branch, J)
    part_out = scatter(rows_product(attended_here, branch_all).astype(bf16), G)
    index = [0] * len(ALL)
    moves = []
    for source in range(n_g * n_j):
        rest = source
        for at in reversed(range(len(ALL))):
            index[at] = rest % size[ALL[at]]
            rest //= size[ALL[at]]
        dp_at, rep_at, zb_at, mb_at, u_at = index
        chunk = (dp_at * size["rep"] + rep_at) * n_mb + mb_at
        moves.append((source, (zb_at * n_u + u_at) * n_g + chunk))
    grad_w_out = lax.ppermute(part_out, ALL, moves).astype(f32)
    part_qkv = owner_rows(rows_product(normed_one, grad_qkv).astype(bf16))
    own_qkv = exchange(scatter(part_qkv, G), J, 0, 0)
    own_qkv = own_qkv.reshape(n_j, rows, 3, cols).transpose(1, 2, 0, 3)
    grad_w_qkv = own_qkv.reshape(rows, 3 * width).astype(f32)

    start = lax.axis_index(ALL) * rows

    def gain_rows(gain, weight, grad):
        total = jnp.sum(weight.astype(f32) * grad, axis=1)
        return total / lax.dynamic_slice_in_dim(gain, start, rows)

    return (
        output[:, None],
        input_grad.astype(f32)[:, None],
        gain_rows(gain_attn, w_qkv, grad_w_qkv),
        grad_w_qkv,
        grad_w_out,
        gain_rows(gain_mlp, w_up, grad_w_up),
        grad_w_up,
        grad_w_down,
    )


def solution(mesh):
    n_dp, n_blk, n_uly = (mesh.shape[name] for name in ("dp", "blk", "ulysses"))
    n_mb = 2
    n_rep = max(1, n_blk * (n_uly // n_mb) // HEADS)
    shape = (n_dp, n_rep, n_blk // n_rep, n_mb, n_uly // n_mb)
    assert math.prod(shape) == mesh.devices.size
    fine = Mesh(mesh.devices.reshape(shape), ALL)
    stream = P(None, "dp", ("rep", "zb", "mb", "u"), None)
    weight = P(ALL, None)
    return jax.shard_map(
        on_device,
        mesh=fine,
        in_specs=(stream, P(), weight, weight, P(), weight, weight, P(None, "dp", None), stream),
        out_specs=(stream, stream, P(ALL), weight, weight, P(ALL), weight, weight),
        check_vma=False,
    )
```

```python
import math

import jax
import jax.numpy as jnp
from jax import lax
from jax.sharding import Mesh
from jax.sharding import PartitionSpec as P

HEADS = 16
HEAD_DIM = 128
epsilon = 1e-05
bf16 = jnp.bfloat16
f32 = jnp.float32

J = ("zb", "u")
G = ("dp", "mb", "rep")
ALL = ("dp", "mb", "rep", "zb", "u")


def normalize(field):
    centered = field - jnp.mean(field, axis=-1, keepdims=True)
    inv_std = lax.rsqrt(jnp.mean(centered * centered, axis=-1, keepdims=True) + epsilon)
    return centered * inv_std, inv_std


def norm_back(grad_out, normed, inv_std, gain_vector):
    scaled = grad_out * gain_vector
    mean_one = jnp.mean(scaled, axis=-1, keepdims=True)
    mean_two = jnp.mean(scaled * normed, axis=-1, keepdims=True)
    return inv_std * (scaled - mean_one - normed * mean_two)


def document_ids(lengths, positions):
    starts = jnp.cumsum(lengths) - lengths
    return jnp.sum((positions[:, None] >= starts[None, 1:]).astype(jnp.int32), axis=1)


def times(left, right):
    return jnp.dot(left, right, preferred_element_type=f32)


def times_transposed(left, right):
    return lax.dot_general(left, right, (((1,), (1,)), ((), ())), preferred_element_type=f32)


def rows_product(left, right):
    return lax.dot_general(left, right, (((0,), (0,)), ((), ())), preferred_element_type=f32)


def gather(field, axes):
    return lax.all_gather(field, axes, axis=0, tiled=True)


def scatter(field, axes):
    return lax.psum_scatter(field, axes, scatter_dimension=0, tiled=True)


def exchange(field, axes, split, concat):
    return lax.all_to_all(field, axes, split, concat, tiled=True)


def pair_swap(field, axis):
    return lax.ppermute(field, axis, [(0, 1), (1, 0)])


def group_bits():
    bits = {}
    for axis in reversed(G):
        if lax.axis_size(axis) > 1:
            assert lax.axis_size(axis) == 2
            bits[axis] = 1 << len(bits)
    return bits


def relative(chunks, bits):
    for axis, bit in bits.items():
        flipped = lax.axis_index(axis) == 1
        chunks = [jnp.where(flipped, chunks[k ^ bit], chunks[k]) for k in range(len(chunks))]
    return chunks


def relative_cols(field, bits):
    return jnp.concatenate(relative(jnp.split(field, 1 << len(bits), axis=1), bits), axis=1)


def spread(block, bits, order):
    blocks = {0: block}
    for axis in order:
        if axis in bits:
            for k in list(blocks):
                blocks[k | bits[axis]] = pair_swap(blocks[k], axis)
    return [blocks[k] for k in range(len(blocks))]


def collect(chunks, bits, order):
    chunks = dict(enumerate(chunks))
    for axis in order:
        if axis in bits:
            bit = bits[axis]
            for k in sorted(chunks, reverse=True):
                if k & bit:
                    came = pair_swap(chunks.pop(k).astype(bf16), axis)
                    chunks[k ^ bit] = chunks[k ^ bit].astype(f32) + came.astype(f32)
    return chunks[0]


def on_device(inputs, gain_attn, w_qkv, w_out, gain_mlp, w_up, w_down, doc_lengths, cotangent):
    size = {name: lax.axis_size(name) for name in ALL}
    bits = group_bits()
    n_g = size["dp"] * size["mb"] * size["rep"]
    n_j = size["zb"] * size["u"]
    rows = w_qkv.shape[0]
    width = rows * n_g * n_j
    rows_down = w_down.shape[0]
    heads_here = HEADS // n_j
    cols = heads_here * HEAD_DIM
    piece = inputs.shape[2]
    tokens = 2 * piece
    group = n_j * tokens
    gather_order = ("mb", "rep", "dp")
    reduce_order = ("dp", "rep", "mb")
    mb_at = lax.axis_index("mb")
    second = mb_at == 1

    def swap_in(field):
        kept = jnp.where(second, field[1, 0], field[0, 0])
        sent = jnp.where(second, field[0, 0], field[1, 0])
        return jnp.concatenate([kept, pair_swap(sent, "mb")])

    def swap_out(field, low):
        kept = field[:piece]
        came = pair_swap(field[piece:].astype(bf16), "mb").astype(low)
        kept = kept.astype(low)
        return jnp.stack([jnp.where(second, came, kept), jnp.where(second, kept, came)])[:, None]

    stream_in = swap_in(inputs).astype(f32)
    qkv_send = w_qkv.reshape(rows, 3, n_j, cols).transpose(2, 0, 1, 3).reshape(n_j * rows, 3 * cols)
    qkv_here = jnp.concatenate(spread(exchange(qkv_send, J, 0, 0), bits, gather_order))
    out_all = gather(w_out, ALL)
    grad_down = swap_in(cotangent)
    cot_all = gather(grad_down, J)
    up_send = w_up.reshape(rows, n_g, n_j, rows_down).transpose(2, 1, 0, 3)
    up_send = [up_send[:, k].reshape(n_j * rows, rows_down) for k in range(n_g)]
    up_send = jnp.concatenate(relative(up_send, bits), axis=1)
    up_blocks = spread(exchange(up_send, J, 0, 0), bits, gather_order)
    slots = [jnp.split(block, n_g, axis=1) for block in up_blocks]
    up_here = jnp.concatenate(
        [jnp.concatenate([slots[k][k ^ slot] for slot in range(n_g)], axis=1) for k in range(n_g)]
    )
    down_here = jnp.concatenate(spread(w_down, bits, gather_order))

    normed_first, inv_first = normalize(stream_in)
    normed_one = gather(relative_cols((normed_first * gain_attn).astype(bf16), bits), J)
    qkv = times(normed_one, qkv_here).astype(bf16)

    place = lax.broadcasted_iota(jnp.int32, (n_j, 2, piece), 0) * piece
    place = place + lax.broadcasted_iota(jnp.int32, place.shape, 2)
    half = (lax.broadcasted_iota(jnp.int32, place.shape, 1) + mb_at) % 2
    place = (place + half * (size["rep"] * n_j * piece)).reshape(group)
    query_pos = place + lax.axis_index("rep") * (n_j * piece)
    key_pos = jnp.concatenate([place + turn * (n_j * piece) for turn in range(size["rep"])])
    lengths = jnp.where(second, doc_lengths[1, 0], doc_lengths[0, 0])
    query_doc = document_ids(lengths, query_pos)
    key_doc = document_ids(lengths, key_pos)
    allowed = (query_doc[:, None] == key_doc[None, :]) & (key_pos[None, :] <= query_pos[:, None])

    heads = qkv.reshape(group, 3, heads_here, HEAD_DIM)
    queries = heads[:, 0]
    keys = heads[:, 1]
    values = heads[:, 2]
    if size["rep"] > 1:
        keys = gather(keys, "rep")
        values = gather(values, "rep")
    score_scale = HEAD_DIM ** (-0.5)
    scores = jnp.einsum("qhd,khd->hqk", queries, keys, preferred_element_type=f32) * score_scale
    scores = jnp.where(allowed[None], scores, -1e30)
    row_max = jnp.max(scores, axis=-1, keepdims=True)
    weights = jnp.exp(scores - row_max)
    probs = weights / jnp.sum(weights, axis=-1, keepdims=True)
    probs_low = probs.astype(bf16)
    attended_full = jnp.einsum("hqk,khd->qhd", probs_low, values, preferred_element_type=f32)
    attended_here = attended_full.reshape(group, cols).astype(bf16)
    attended = exchange(attended_here, J, 0, 1)
    middle = stream_in + times(attended, out_all)

    normed_second, inv_second = normalize(middle)
    normed_two = gather(relative_cols((normed_second * gain_mlp).astype(bf16), bits), J)
    up_proj = times(normed_two, up_here)
    activated_full, gelu_back = jax.vjp(lambda field: jax.nn.gelu(field, approximate=True), up_proj)
    activated = activated_full.astype(bf16)
    grad_up = gelu_back(times_transposed(cot_all, down_here))[0].astype(bf16)
    grad_two = scatter(times_transposed(grad_up, up_here).astype(bf16), J)
    grad_two = relative_cols(grad_two.astype(f32), bits)
    grad_middle = grad_down.astype(f32) + norm_back(grad_two, normed_second, inv_second, gain_mlp)
    grad_branch = grad_middle.astype(bf16)
    grad_attended = times_transposed(grad_branch, out_all).astype(bf16)
    grad_out = exchange(grad_attended, J, 1, 0).reshape(group, heads_here, HEAD_DIM)
    row_dots = jnp.sum(grad_out.astype(f32) * attended_full, axis=-1).T
    grad_values = jnp.einsum("hqk,qhd->khd", probs_low, grad_out, preferred_element_type=f32)
    grad_probs = jnp.einsum("qhd,khd->hqk", grad_out, values, preferred_element_type=f32)
    grad_scores = (probs * (grad_probs - row_dots[:, :, None])).astype(bf16)
    grad_queries = jnp.einsum("hqk,khd->qhd", grad_scores, keys, preferred_element_type=f32)
    grad_keys = jnp.einsum("hqk,qhd->khd", grad_scores, queries, preferred_element_type=f32)
    grad_queries = (grad_queries * score_scale).astype(bf16)
    grad_keys = (grad_keys * score_scale).astype(bf16)
    grad_values = grad_values.astype(bf16)
    if size["rep"] > 1:
        grad_keys = scatter(grad_keys, "rep")
        grad_values = scatter(grad_values, "rep")
    grad_qkv = jnp.stack([grad_queries, grad_keys, grad_values], axis=1).reshape(group, 3 * cols)
    grad_one = scatter(times_transposed(grad_qkv, qkv_here).astype(bf16), J)
    grad_one = relative_cols(grad_one.astype(f32), bits)
    input_grad = grad_middle + norm_back(grad_one, normed_first, inv_first, gain_attn)
    input_grad = swap_out(input_grad, f32)
    result = middle + scatter(times(activated, down_here).astype(bf16), J).astype(f32)
    output = swap_out(result, bf16)

    def parts(left, right):
        return [rows_product(chunk, right) for chunk in jnp.split(left, n_g, axis=1)]

    grad_w_down = collect(parts(activated, cot_all), bits, reduce_order)
    part_up = []
    for k, part in enumerate(parts(normed_two, grad_up)):
        slot = jnp.split(part if k == 0 else part.astype(bf16), n_g, axis=1)
        part_up.append(jnp.concatenate([slot[k ^ at] for at in range(n_g)], axis=1))
    own_up = exchange(collect(part_up, bits, reduce_order).astype(bf16), J, 0, 0)
    own_up = own_up.reshape(n_j, rows, n_g, rows_down)
    own_up = jnp.stack(relative([own_up[:, :, k] for k in range(n_g)], bits))
    grad_w_up = own_up.transpose(2, 0, 1, 3).reshape(rows, n_g * n_j * rows_down).astype(f32)
    branch_all = gather(grad_branch, J)
    part_out = rows_product(attended_here, branch_all)
    part_out = collect(relative(jnp.split(part_out, n_g), bits), bits, reduce_order)
    moves = [(g * n_j + j, j * n_g + g) for g in range(n_g) for j in range(n_j)]
    grad_w_out = lax.ppermute(part_out.astype(bf16), ALL, moves).astype(f32)
    own_qkv = collect(parts(normed_one, grad_qkv), bits, reduce_order).astype(bf16)
    own_qkv = exchange(own_qkv, J, 0, 0).reshape(n_j, rows, 3, cols).transpose(1, 2, 0, 3)
    grad_w_qkv = own_qkv.reshape(rows, 3 * width).astype(f32)

    start = lax.axis_index(ALL) * rows

    def gain_rows(gain, weight, grad):
        total = jnp.sum(weight.astype(f32) * grad, axis=1)
        return total / lax.dynamic_slice_in_dim(gain, start, rows)

    return (
        output,
        input_grad,
        gain_rows(gain_attn, w_qkv, grad_w_qkv),
        grad_w_qkv,
        grad_w_out,
        gain_rows(gain_mlp, w_up, grad_w_up),
        grad_w_up,
        grad_w_down,
    )


def solution(mesh):
    n_dp, n_blk, n_uly = (mesh.shape[name] for name in ("dp", "blk", "ulysses"))
    n_mb = 2
    n_rep = max(1, n_blk * n_uly // n_mb // HEADS)
    shape = (n_dp, n_mb, n_rep, n_blk // (n_mb * n_rep), n_uly)
    assert math.prod(shape) == mesh.devices.size
    fine = Mesh(mesh.devices.reshape(shape), ALL)
    stream = P(None, "dp", ("mb", "rep", "zb", "u"), None)
    weight = P(ALL, None)
    return jax.shard_map(
        on_device,
        mesh=fine,
        in_specs=(stream, P(), weight, weight, P(), weight, weight, P(None, "dp", None), stream),
        out_specs=(stream, stream, P(ALL), weight, weight, P(ALL), weight, weight),
        check_vma=False,
    )
```

```python
import math

import jax
import jax.numpy as jnp
from jax import lax
from jax.sharding import Mesh
from jax.sharding import PartitionSpec as P

HEADS = 16
HEAD_DIM = 128
epsilon = 1e-05
bf16 = jnp.bfloat16
f32 = jnp.float32

J = ("zb", "uo", "ui")
G = ("dp", "mb", "rep")
ALL = ("dp", "mb", "rep", "zb", "uo", "ui")


def normalize(field):
    centered = field - jnp.mean(field, axis=-1, keepdims=True)
    inv_std = lax.rsqrt(jnp.mean(centered * centered, axis=-1, keepdims=True) + epsilon)
    return centered * inv_std, inv_std


def norm_back(grad_out, normed, inv_std, gain_vector):
    scaled = grad_out * gain_vector
    mean_one = jnp.mean(scaled, axis=-1, keepdims=True)
    mean_two = jnp.mean(scaled * normed, axis=-1, keepdims=True)
    return inv_std * (scaled - mean_one - normed * mean_two)


def document_ids(lengths, positions):
    starts = jnp.cumsum(lengths) - lengths
    return jnp.sum((positions[:, None] >= starts[None, 1:]).astype(jnp.int32), axis=1)


def times(left, right):
    return jnp.dot(left, right, preferred_element_type=f32)


def times_transposed(left, right):
    return lax.dot_general(left, right, (((1,), (1,)), ((), ())), preferred_element_type=f32)


def rows_product(left, right):
    return lax.dot_general(left, right, (((0,), (0,)), ((), ())), preferred_element_type=f32)


def gather(field, axes):
    return lax.all_gather(field, axes, axis=0, tiled=True)


def scatter(field, axes):
    return lax.psum_scatter(field, axes, scatter_dimension=0, tiled=True)


def exchange(field, axes, split, concat):
    return lax.all_to_all(field, axes, split, concat, tiled=True)


def pair_swap(field, axis):
    return lax.ppermute(field, axis, [(0, 1), (1, 0)])


def group_bits():
    bits = {}
    for axis in reversed(G):
        if lax.axis_size(axis) > 1:
            assert lax.axis_size(axis) == 2
            bits[axis] = 1 << len(bits)
    return bits


def relative(chunks, bits):
    for axis, bit in bits.items():
        flipped = lax.axis_index(axis) == 1
        chunks = [jnp.where(flipped, chunks[k ^ bit], chunks[k]) for k in range(len(chunks))]
    return chunks


def relative_cols(field, bits):
    return jnp.concatenate(relative(jnp.split(field, 1 << len(bits), axis=1), bits), axis=1)


def spread(block, bits):
    blocks = {0: block}
    for axis in ("mb", "rep", "dp"):
        if axis in bits:
            for k in list(blocks):
                blocks[k | bits[axis]] = pair_swap(blocks[k], axis)
    return [blocks[k] for k in range(len(blocks))]


def placed(blocks, own):
    rows = blocks[0].shape[0]
    out = jnp.zeros((len(blocks) * rows,) + blocks[0].shape[1:], blocks[0].dtype)
    for k, block in enumerate(blocks):
        out = lax.dynamic_update_slice_in_dim(out, block, (own ^ k) * rows, 0)
    return out


def collect(part, bits, relative_order):
    axes = [axis for axis in G if axis in bits]
    size = part(None, None) >> 1
    field = None
    for axis in axes:
        me = lax.axis_index(axis)
        if relative_order:
            keep_at, send_at = 0, size
        else:
            keep_at, send_at = me * size, (1 - me) * size
        if field is None:
            sent = part(send_at, size).astype(bf16)
        else:
            sent = lax.dynamic_slice_in_dim(field, send_at, size).astype(bf16)
        came = pair_swap(sent, axis).astype(f32)
        if field is None:
            field = part(keep_at, size) + came
        else:
            field = lax.dynamic_slice_in_dim(field, keep_at, size) + came
        size >>= 1
    return field


def on_device(inputs, gain_attn, w_qkv, w_out, gain_mlp, w_up, w_down, doc_lengths, cotangent):
    size = {name: lax.axis_size(name) for name in ALL}
    bits = group_bits()
    n_g = size["dp"] * size["mb"] * size["rep"]
    n_j = size["zb"] * size["uo"] * size["ui"]
    rows = w_qkv.shape[0]
    width = rows * n_g * n_j
    rows_down = w_down.shape[0]
    heads_here = HEADS // n_j
    cols = heads_here * HEAD_DIM
    pieces = size["ui"]
    sets = n_j // pieces
    own = sum(lax.axis_index(axis) * bit for axis, bit in bits.items())
    piece = inputs.shape[2]
    tokens = 2 * piece
    group = n_j * tokens
    mb_at = lax.axis_index("mb")
    second = mb_at == 1

    def swap_in(field):
        kept = jnp.where(second, field[1, 0], field[0, 0])
        sent = jnp.where(second, field[0, 0], field[1, 0])
        return jnp.concatenate([kept, pair_swap(sent, "mb")])

    def swap_out(field, low):
        kept = field[:piece]
        came = pair_swap(field[piece:].astype(bf16), "mb").astype(low)
        kept = kept.astype(low)
        return jnp.stack([jnp.where(second, came, kept), jnp.where(second, kept, came)])[:, None]

    stream_in = swap_in(inputs).astype(f32)
    out_blocks = spread(w_out, bits)
    qkv_send = w_qkv.reshape(rows, 3, pieces, heads_here, sets, HEAD_DIM).transpose(4, 2, 0, 1, 3, 5)
    qkv_part = exchange(qkv_send.reshape(n_j * rows, 3 * cols), J, 0, 0)
    qkv_here = jnp.concatenate(spread(qkv_part, bits))
    up_send = w_up.reshape(rows, n_g, n_j, rows_down).transpose(2, 0, 1, 3)
    up_part = exchange(up_send.reshape(n_j * rows, n_g * rows_down), J, 0, 0)
    up_here = jnp.concatenate(spread(up_part, bits))
    down_here = placed(spread(w_down, bits), own)
    grad_down = swap_in(cotangent)
    cot_all = gather(grad_down, J)
    out_here = exchange(placed(out_blocks, own), "ui", 0, 0)
    out_here = out_here.reshape(pieces, heads_here, rows, width).transpose(1, 0, 2, 3).reshape(cols, width)

    normed_first, inv_first = normalize(stream_in)
    normed_one = relative_cols((normed_first * gain_attn).astype(bf16), bits)
    normed_one = gather(normed_one, J)
    qkv = times(normed_one, qkv_here).astype(bf16)

    place = lax.broadcasted_iota(jnp.int32, (n_j, 2, piece), 0) * piece
    place = place + lax.broadcasted_iota(jnp.int32, place.shape, 2)
    half = (lax.broadcasted_iota(jnp.int32, place.shape, 1) + mb_at) % 2
    place = (place + half * (size["rep"] * n_j * piece)).reshape(group)
    query_pos = place + lax.axis_index("rep") * (n_j * piece)
    key_pos = jnp.concatenate([place + turn * (n_j * piece) for turn in range(size["rep"])])
    lengths = jnp.where(second, doc_lengths[1, 0], doc_lengths[0, 0])
    query_doc = document_ids(lengths, query_pos)
    key_doc = document_ids(lengths, key_pos)
    allowed = (query_doc[:, None] == key_doc[None, :]) & (key_pos[None, :] <= query_pos[:, None])

    heads = qkv.reshape(group, 3, heads_here, HEAD_DIM)
    queries = heads[:, 0]
    keys = heads[:, 1]
    values = heads[:, 2]
    if size["rep"] > 1:
        keys = gather(keys, "rep")
        values = gather(values, "rep")
    score_scale = HEAD_DIM ** (-0.5)
    scores = jnp.einsum("qhd,khd->hqk", queries, keys, preferred_element_type=f32) * score_scale
    scores = jnp.where(allowed[None], scores, -1e30)
    row_max = jnp.max(scores, axis=-1, keepdims=True)
    weights = jnp.exp(scores - row_max)
    probs = weights / jnp.sum(weights, axis=-1, keepdims=True)
    probs_low = probs.astype(bf16)
    attended_full = jnp.einsum("hqk,khd->qhd", probs_low, values, preferred_element_type=f32)
    attended_here = attended_full.reshape(group, cols).astype(bf16)
    branch = times(attended_here, out_here).astype(bf16)
    middle = stream_in + scatter(branch, J).astype(f32)

    normed_second, inv_second = normalize(middle)
    normed_two = relative_cols((normed_second * gain_mlp).astype(bf16), bits)
    normed_two = gather(normed_two, J)
    up_proj = times(normed_two, up_here)
    activated_full, gelu_back = jax.vjp(lambda field: jax.nn.gelu(field, approximate=True), up_proj)
    activated = activated_full.astype(bf16)
    grad_up = gelu_back(times_transposed(cot_all, down_here))[0].astype(bf16)
    grad_two = times_transposed(grad_up, up_here).astype(bf16)
    grad_two = scatter(grad_two, J)
    grad_two = relative_cols(grad_two.astype(f32), bits)
    grad_middle = grad_down.astype(f32) + norm_back(grad_two, normed_second, inv_second, gain_mlp)
    grad_branch = grad_middle.astype(bf16)
    branch_all = gather(grad_branch, J)
    grad_out = times_transposed(branch_all, out_here).astype(bf16).reshape(group, heads_here, HEAD_DIM)
    row_dots = jnp.sum(grad_out.astype(f32) * attended_full, axis=-1).T
    grad_values = jnp.einsum("hqk,qhd->khd", probs_low, grad_out, preferred_element_type=f32)
    grad_probs = jnp.einsum("qhd,khd->hqk", grad_out, values, preferred_element_type=f32)
    grad_scores = (probs * (grad_probs - row_dots[:, :, None])).astype(bf16)
    grad_queries = jnp.einsum("hqk,khd->qhd", grad_scores, keys, preferred_element_type=f32)
    grad_keys = jnp.einsum("hqk,qhd->khd", grad_scores, queries, preferred_element_type=f32)
    grad_queries = (grad_queries * score_scale).astype(bf16)
    grad_keys = (grad_keys * score_scale).astype(bf16)
    grad_values = grad_values.astype(bf16)
    if size["rep"] > 1:
        grad_keys = scatter(grad_keys, "rep")
        grad_values = scatter(grad_values, "rep")
    grad_qkv = jnp.stack([grad_queries, grad_keys, grad_values], axis=1).reshape(group, 3 * cols)
    grad_one = times_transposed(grad_qkv, qkv_here).astype(bf16)
    grad_one = scatter(grad_one, J)
    grad_one = relative_cols(grad_one.astype(f32), bits)
    input_grad = grad_middle + norm_back(grad_one, normed_first, inv_first, gain_attn)
    input_grad = swap_out(input_grad, f32)
    result = times(activated, down_here).astype(bf16)
    result = middle + scatter(result, J).astype(f32)
    output = swap_out(result, bf16)

    def part_of(left, right):
        def part(start, count):
            if start is None:
                return left.shape[1]
            return rows_product(lax.dynamic_slice_in_dim(left, start, count, 1), right)

        return part

    grad_w_down = collect(part_of(activated, cot_all), bits, False)
    own_up = collect(part_of(normed_two, grad_up), bits, True).astype(bf16)
    own_up = exchange(own_up, J, 0, 0).reshape(n_j, rows, n_g, rows_down)
    grad_w_up = own_up.transpose(1, 2, 0, 3).reshape(rows, n_g * n_j * rows_down).astype(f32)
    part_out = rows_product(attended_here, branch_all).astype(bf16)
    part_out = part_out.reshape(heads_here, pieces, rows, width).transpose(1, 0, 2, 3)
    part_out = exchange(part_out.reshape(n_g * rows, width), "ui", 0, 0)

    def part_of_out(start, count):
        return part_out.shape[0] if start is None else lax.dynamic_slice_in_dim(part_out, start, count).astype(f32)

    grad_w_out = collect(part_of_out, bits, False)
    own_qkv = collect(part_of(normed_one, grad_qkv), bits, True).astype(bf16)
    own_qkv = exchange(own_qkv, J, 0, 0).reshape(sets, pieces, rows, 3, heads_here, HEAD_DIM)
    grad_w_qkv = own_qkv.transpose(2, 3, 1, 4, 0, 5).reshape(rows, 3 * width).astype(f32)

    start = lax.axis_index(ALL) * rows

    def gain_rows(gain, weight, grad):
        total = jnp.sum(weight.astype(f32) * grad, axis=1)
        return total / lax.dynamic_slice_in_dim(gain, start, rows)

    return (
        output,
        input_grad,
        gain_rows(gain_attn, w_qkv, grad_w_qkv),
        grad_w_qkv,
        grad_w_out,
        gain_rows(gain_mlp, w_up, grad_w_up),
        grad_w_up,
        grad_w_down,
    )


def solution(mesh):
    n_dp, n_blk, n_uly = (mesh.shape[name] for name in ("dp", "blk", "ulysses"))
    n_mb = 2
    n_rep = max(1, n_blk * n_uly // n_mb // HEADS)
    pieces = mesh.devices.size // HEADS
    shape = (n_dp, n_mb, n_rep, n_blk // (n_mb * n_rep), n_uly // pieces, pieces)
    assert math.prod(shape) == mesh.devices.size
    fine = Mesh(mesh.devices.reshape(shape), ALL)
    stream = P(None, "dp", ("mb", "rep", "zb", "uo", "ui"), None)
    weight = P(ALL, None)

    return jax.shard_map(
        on_device,
        mesh=fine,
        in_specs=(stream, P(), weight, weight, P(), weight, weight, P(None, "dp", None), stream),
        out_specs=(stream, stream, P(ALL), weight, weight, P(ALL), weight, weight),
        check_vma=False,
    )
```
